32 devices in a mesh: param: 16 (over z, y, x), trace: 2 (over core).
Axes of the slice: x: 2, y: 2, z: 4, core: 2. Of those that a mesh axis runs over, the one named last changes fastest.
Arguments:
- grads: bfloat16 [8, 16777216], P('trace', 'param'), may hold values from -6 to 6
- signs: int32 [16777216], P('param'), may hold values 0 or 1
- kept: int32 [512], replicated, may hold values from 0 to 131071, as said below
Outputs:
- features: float32 [8, 65536], P(None, ('param', 'trace'))
The draws below stay inside these ranges and needn't reach their ends.
Inputs may be any that keep to these rules, and one draw needn't show every extreme that they name: `kept`: 512 distinct block numbers.
All inputs are finite; a program needn't handle non-finite values. No bound on the sum of `signs` on one device may be relied on, other than what follows from the above.
Results may differ from the reference program's by a relative error of at most 0.0003.
Values sent between devices are 32-bit elements; how exact they have to be, the bound alone decides.
A program may use at most 192 MiB of HBM per device.

```python
import jax
import jax.numpy as jnp
from jax import lax

D = 4096
BLOCK = 128
KEEP = 512
TRACES = 8
LENGTH = 16777216
N_PARAM = 16


def draw_kept(key, part):
    all_blocks = D * D // BLOCK
    key_level = jax.random.fold_in(key, 11)
    key_jitter = jax.random.fold_in(key, 23)
    positions = jnp.arange(all_blocks, dtype=jnp.int32)
    levels = jax.random.randint(key_level, (64,), 0, 4, dtype=jnp.int32)
    level_here = levels[positions // (all_blocks // 64)]
    jitter = jax.random.randint(key_jitter, (all_blocks,), 0, 1024, dtype=jnp.int32)
    scores = (jitter + 256 * level_here) * all_blocks + positions
    edges = (positions == 0) | (positions == all_blocks - 1)
    scores = jnp.where(edges, 2 ** 30 + positions, scores)
    _, chosen = lax.top_k(scores, KEEP)
    return chosen.astype(jnp.int32)


def set_ends(entries, rng, least, high):
    spot = [jax.random.randint(jax.random.fold_in(rng, axis), (), 0, length) for axis, length in enumerate(entries.shape)]
    longest = entries.shape.index(max(entries.shape))
    neighbour = spot[:longest] + [(spot[longest] + 1) % entries.shape[longest]] + spot[longest + 1:]
    return entries.at[tuple(spot)].set(least).at[tuple(neighbour)].set(high)


def block_levels(key, dims, shards, low, top_value):
    def one(axis_at, blocks):
        heights = jax.random.uniform(jax.random.fold_in(jax.random.fold_in(key, 6), axis_at), (blocks,), jnp.float32, low / len(shards), top_value / len(shards))
        return jnp.repeat(jnp.exp(heights), dims[axis_at] // blocks).reshape((-1,) + (1,) * (len(dims) - axis_at - 1))

    loudness = one(*shards[0])
    for cut in shards[1:]:
        loudness = loudness * one(*cut)
    return loudness


def gaussian(key, shape, scale, reach, pieces=(), kind=jnp.bfloat16):
    factor_of = block_levels(key, shape, pieces, -0.22, 0.18) if pieces else 1.0
    result = jax.random.normal(key, shape, jnp.float32) * scale * factor_of
    return jnp.minimum(jnp.maximum(result, -reach), reach).astype(kind)


def setup_inputs(seed: int = 0) -> dict:
    key_list = jax.random.split(jax.random.key(seed), 4)
    grads = gaussian(key_list[0], (TRACES, LENGTH), 1.0, 6.0, ((0, 2), (1, 16)))
    signs = set_ends((jax.random.randint(key_list[1], (LENGTH,), 0, 2) < 1).astype(jnp.int32), jax.random.fold_in(key_list[1], 1), 0, 1)
    kept = draw_kept(jax.random.fold_in(key_list[3], 71), 0)
    return {"grads": grads, "signs": signs, "kept": kept}


def parity_signs(row_values, col_values, bit_count):
    intersection = row_values[:, None] & col_values[None, :]
    parity = jnp.zeros(intersection.shape, jnp.int32)
    for bit_number in range(bit_count):
        parity = parity + ((intersection >> bit_number) & 1)
    return 1 - 2 * (parity % 2)


def reference(grads, signs, kept):
    length = D * D
    local_size = length // N_PARAM
    left_size = 2 ** ((local_size.bit_length() - 1) // 2)
    right_size = local_size // left_size
    left_table = parity_signs(jnp.arange(left_size, dtype=jnp.int32), jnp.arange(left_size, dtype=jnp.int32), left_size.bit_length()).astype(jnp.float32)
    right_table = parity_signs(jnp.arange(right_size, dtype=jnp.int32), jnp.arange(right_size, dtype=jnp.int32), right_size.bit_length()).astype(jnp.float32)
    blocks_dev = local_size // BLOCK
    region = (kept // blocks_dev).astype(jnp.int32)
    within = (kept % blocks_dev).astype(jnp.int32)
    mixing = parity_signs(region, jnp.arange(N_PARAM, dtype=jnp.int32), N_PARAM.bit_length()).astype(jnp.float32)

    def one_trace(trace_row):
        signed = jnp.where(signs == 1, trace_row, -trace_row).astype(jnp.float32).reshape(N_PARAM, left_size, right_size)
        half_done = jnp.einsum('ij,ajk->aik', left_table, signed, precision=lax.Precision.HIGHEST)
        whole = jnp.einsum('aik,kl->ail', half_done, right_table, precision=lax.Precision.HIGHEST)
        picked = whole.reshape(N_PARAM, blocks_dev, BLOCK)[:, within, :]
        mixed = jnp.einsum('fa,afc->fc', mixing, picked, precision=lax.Precision.HIGHEST)
        return (mixed / D).reshape(KEEP * BLOCK)

    return lax.map(one_trace, grads)
```

```python
import functools

import jax
import jax.numpy as jnp
from jax import lax
from jax.experimental import pallas as pl
from jax.experimental.pallas import tpu as pltpu
from jax.sharding import PartitionSpec as P

D = 4096
BLOCK = 128
UNITS = 16
CHUNKS = (1, 2, 3, 4, 6)
BANDS = 4
MESH = pl.DeviceIdType.MESH


def parity(value, bits):
    shift = 1 << (bits - 1).bit_length()
    while shift > 1:
        shift //= 2
        value = value ^ (value >> shift)
    return value & 1


def sign_of(value, bits):
    return (1 - 2 * parity(value, bits)).astype(jnp.float32).astype(jnp.bfloat16)


def bit_sign(value, bit):
    return (1 - 2 * ((value >> (bit.bit_length() - 1)) & 1)).astype(jnp.float32).astype(jnp.bfloat16)


def cut_of(groups):
    bits = groups.bit_length() - 1
    minor = bits // 3
    return 2 ** (bits - 2 * minor), 2 ** minor, 2 ** minor


def chunk_copies(k, x_hbm, s_hbm, x_ref, s_ref, load_sem):
    unit = s_ref.shape[0] // UNITS
    traces = x_ref.shape[0] // s_ref.shape[0]
    low, size = sum(CHUNKS[:k]) * unit, CHUNKS[k] * unit
    return (
        pltpu.make_async_copy(
            x_hbm.at[pl.ds(low * traces, size * traces)], x_ref.at[pl.ds(low * traces, size * traces)],
            load_sem.at[2 * k],
        ),
        pltpu.make_async_copy(
            s_hbm.at[pl.ds(low, size)], s_ref.at[pl.ds(low, size)], load_sem.at[2 * k + 1]
        ),
    )


def visit_order(count):
    return [0, count - 1, *range(1, count - 1)] if count > 1 else [0]


def fill_tables(kept_ref, low_ref, high_ref, order):
    unit = low_ref.shape[1]
    kept = jnp.concatenate(
        [jnp.broadcast_to(kept_ref[n:n + 1, :], (BLOCK, BLOCK)).T for n in order], axis=0
    )
    lane = lax.broadcasted_iota(jnp.int32, kept.shape, 1)
    tables = [sign_of(kept & lane, 7)]
    while len(tables) * BLOCK < unit:
        bit = bit_sign(kept, len(tables) * BLOCK)
        tables += [table * bit for table in tables]
    for k, table in enumerate(tables):
        low_ref[:, k * BLOCK:(k + 1) * BLOCK] = table
    region = UNITS * unit
    own = (kept >> (region.bit_length() - 1)) & lax.axis_index("param")
    highs = [sign_of(own, 8)]
    while len(highs) < UNITS:
        bit = bit_sign(kept, len(highs) * unit)
        highs += [high * bit for high in highs]
    for n, high in enumerate(highs):
        high_ref[n] = high


def load_chunk(k, loads, x_ref, s_ref):
    unit = s_ref.shape[0] // UNITS
    traces = x_ref.shape[0] // s_ref.shape[0]
    for copy in loads:
        copy.wait()
    low, size = sum(CHUNKS[:k]) * unit, CHUNKS[k] * unit
    sign = (2 * s_ref[pl.ds(low, size), :] - 1).astype(jnp.float32).astype(jnp.bfloat16)
    return jnp.concatenate(
        [x_ref[pl.ds(low * traces + t, size, stride=traces), :] * sign for t in range(traces)], axis=1
    )


def add_chunk(band, bands, k, signed, low_ref, high_ref, sums):
    unit = low_ref.shape[1]
    size = low_ref.shape[0] // bands
    rows = slice(band * size, (band + 1) * size)
    first = sum(CHUNKS[:k])
    table = jnp.concatenate(
        [
            low_ref[rows, :] * jnp.concatenate([high_ref[n, rows, :]] * (unit // BLOCK), axis=1)
            for n in range(first, first + CHUNKS[k])
        ],
        axis=1,
    )
    part = jnp.dot(table, signed, preferred_element_type=jnp.float32)
    if k == 0:
        sums[rows, :] = part
    else:
        sums[rows, :] += part


def fused_kernel(
    cut, kept_ref, x_hbm, s_hbm, o_ref, x_ref, s_ref, load_sem, high_ref, low_ref, sums_ref, *rest
):
    recv, held, fin_ref = rest[0:4], rest[4:8], rest[8]
    send_sem, recv_sem, last_send_sem, last_recv_sem = rest[9:]
    loads = [chunk_copies(k, x_hbm, s_hbm, x_ref, s_ref, load_sem) for k in range(len(CHUNKS))]
    for pair in loads:
        for copy in pair:
            copy.start()

    own = lax.axis_index("param")
    core = lax.axis_index("trace")
    spans = (cut[1] * cut[2], cut[2], 1)
    place = tuple((own // spans[d]) % cut[d] for d in range(3))

    def peer(d, offset):
        there = lax.rem(place[d] + offset, cut[d])
        return there, own + (there - place[d]) * spans[d]

    barrier = pltpu.get_barrier_semaphore()
    greeted = []
    for d in range(3):
        for offset in range(1, cut[d]):
            for other in range(2 if d == 0 else 1):
                greeted.append({"param": peer(d, offset)[1], "trace": 1 - core if other else core})
    greeted.append({"param": own, "trace": 1 - core})
    for device in greeted:
        pl.semaphore_signal(barrier, inc=1, device_id=device, device_id_type=MESH)

    rows, width = sums_ref.shape[3], sums_ref.shape[4]
    half = width // 2
    lanes = [pl.ds(0, half), pl.ds(half, half)]
    order = ((2, 1), (1, 2))
    keep = kept_ref.shape[0] * BLOCK
    sums = sums_ref.reshape(keep, width)

    visit = visit_order(cut[0])

    sent = []

    def copy_to(src, dst, device, which):
        copy = pltpu.make_async_remote_copy(
            src_ref=src, dst_ref=dst, send_sem=send_sem.at[which], recv_sem=recv_sem.at[which],
            device_id={"param": device}, device_id_type=MESH,
        )
        copy.start()
        sent.append(copy)
        return copy

    span = [cut[order[h][0]] - 1 + cut[order[h][1]] - 1 for h in range(2)]
    base = [[j * sum(span) + h * span[0] for h in range(2)] for j in range(cut[0])]
    flying = {}

    def piece(ref, axis, index):
        return ref.at[(slice(None),) * axis + (index,)]

    def stage_one(j, h):
        a = order[h][0]
        view = sums_ref.at[j, :, :, :, lanes[h]]
        flying[j, h] = []
        for offset in range(1, cut[a]):
            there, device = peer(a, offset)
            flying[j, h].append(copy_to(
                piece(view, a - 1, there), recv[h].at[j, offset - 1], device, base[j][h] + offset - 1
            ))

    def stage_two(j, h):
        a, b = order[h]
        total = piece(sums_ref.at[j, :, :, :, lanes[h]], a - 1, place[a])[...]
        for offset in range(1, cut[a]):
            flying[j, h][offset - 1].wait_recv()
            total = total + recv[h][j, offset - 1]
        held[h][j] = total
        flying[j, h] = []
        for offset in range(1, cut[b]):
            there, device = peer(b, offset)
            flying[j, h].append(copy_to(
                held[h].at[j, there], recv[2 + h].at[j, offset - 1], device,
                base[j][h] + cut[a] - 1 + offset - 1,
            ))

    share = rows // 2
    whole = share % 8 != 0
    here = fin_ref.shape[2]
    last = []

    def last_copy(j, h, to_core, z, from_core, device, which):
        return pltpu.make_async_remote_copy(
            src_ref=held[2 + h].at[j] if whole else held[2 + h].at[j, pl.ds(to_core * share, share)],
            dst_ref=fin_ref.at[z, from_core, :, lanes[h]],
            send_sem=last_send_sem.at[which],
            recv_sem=last_recv_sem.at[(z * 2 + from_core) * 2 + h],
            device_id=device,
            device_id_type=MESH,
        )

    def stage_three(j, h):
        a, b = order[h]
        total = held[h][j, place[b]]
        for offset in range(1, cut[b]):
            flying[j, h][offset - 1].wait_recv()
            total = total + recv[2 + h][j, offset - 1]
        held[2 + h][j] = total
        mine = place[0] == visit[j]
        target = own + (visit[j] - place[0]) * spans[0]
        first = (j * 2 + h) * 2
        same = last_copy(j, h, core, place[0], core, {"param": target, "trace": core}, first)
        cross = last_copy(j, h, 1 - core, place[0], core, {"param": target, "trace": 1 - core}, first + 1)
        last.append((mine, same, cross))
        cross.start()

        @pl.when(jnp.logical_not(mine))
        def _():
            same.start()

    fill_tables(kept_ref, low_ref, high_ref, visit)
    for k in range(len(CHUNKS) - 1):
        signed = load_chunk(k, loads[k], x_ref, s_ref)
        add_chunk(0, 1, k, signed, low_ref, high_ref, sums)
    signed = load_chunk(len(CHUNKS) - 1, loads[-1], x_ref, s_ref)
    pl.semaphore_wait(barrier, len(greeted))
    ahead = cut[0] // BANDS
    for band in range(BANDS):
        add_chunk(band, BANDS, len(CHUNKS) - 1, signed, low_ref, high_ref, sums)
        if band == 0:
            for j in range(ahead):
                for h in range(2):
                    stage_one(j, h)
    for h in range(2):
        stage_one(ahead, h)
    ahead += 1
    for step in range(cut[0] + 1):
        if step < cut[0]:
            for h in range(2):
                stage_two(step, h)
            if step + ahead < cut[0]:
                for h in range(2):
                    stage_one(step + ahead, h)
        if step >= 1:
            for h in range(2):
                stage_three(step - 1, h)

    at = sum(n * (place[0] == visit[n]).astype(jnp.int32) for n in range(cut[0]))
    for h in range(2):
        for c in range(2):
            @pl.when(core == c)
            def _():
                part = held[2 + h][at]
                fin_ref[place[0], c, :, lanes[h]] = part if whole else part[c * share:(c + 1) * share]

    for z_offset in range(cut[0]):
        z = lax.rem(place[0] + z_offset, cut[0])
        for c in range(2):
            for h in range(2):
                copy = pltpu.make_async_remote_copy(
                    src_ref=fin_ref.at[z, c, :, lanes[h]], dst_ref=fin_ref.at[z, c, :, lanes[h]],
                    send_sem=last_send_sem.at[0], recv_sem=last_recv_sem.at[(z * 2 + c) * 2 + h],
                    device_id={"param": own, "trace": 1 - core}, device_id_type=MESH,
                )
                if z_offset == 0:
                    pl.when(core != c)(copy.wait_recv)
                else:
                    copy.wait_recv()
    both = []
    for c in range(2):
        total = fin_ref[0, c]
        for z in range(1, cut[0]):
            total = total + fin_ref[z, c]
        if whole:
            total = jnp.where(core == 0, total[0:share], total[share:2 * share])
        both.append(total)
    local = width // BLOCK
    for c in range(2):
        for t in range(local):
            o_ref[pl.ds(c * local + t, share, stride=2 * local), :] = both[c][:, t * BLOCK:(t + 1) * BLOCK]
    index = lax.broadcasted_iota(jnp.int32, (BLOCK, BLOCK), 0) & lax.broadcasted_iota(jnp.int32, (BLOCK, BLOCK), 1)
    table = (1 - 2 * parity(index, 7)).astype(jnp.float32) * (1.0 / D)
    o_ref[...] = jnp.dot(
        o_ref[...], table, precision=lax.Precision.HIGHEST, preferred_element_type=jnp.float32
    )
    for copy in sent:
        copy.wait_send()
    for mine, same, cross in last:
        cross.wait_send()
        pl.when(jnp.logical_not(mine))(same.wait_send)


def per_device(grads, signs, kept):
    traces, local_size = grads.shape
    groups = lax.axis_size("param")
    keep, width = kept.shape[0], traces * BLOCK
    blocks = local_size // BLOCK
    unit = blocks // UNITS
    x = grads.reshape(traces, blocks, BLOCK).transpose(1, 0, 2).reshape(blocks * traces, BLOCK)
    s = signs.reshape(blocks, BLOCK)
    cut = cut_of(groups)
    rows = keep // groups
    share = rows // 2
    lanes = width // 2
    order = ((2, 1), (1, 2))
    recv_one = [pltpu.VMEM((cut[0], max(cut[a] - 1, 1), cut[b], rows, lanes), jnp.float32) for a, b in order]
    recv_two = [pltpu.VMEM((cut[0], max(cut[b] - 1, 1), rows, lanes), jnp.float32) for a, b in order]
    held_one = [pltpu.VMEM((cut[0], cut[b], rows, lanes), jnp.float32) for a, b in order]
    held_two = [pltpu.VMEM((cut[0], rows, lanes), jnp.float32) for _ in order]
    copies = cut[0] * 2 * (cut[1] + cut[2] - 2)
    out = pl.pallas_call(
        functools.partial(fused_kernel, cut),
        out_shape=jax.ShapeDtypeStruct((share * 2 * width // BLOCK, BLOCK), jnp.float32),
        in_specs=[
            pl.BlockSpec(memory_space=pltpu.VMEM),
            pl.BlockSpec(memory_space=pl.ANY),
            pl.BlockSpec(memory_space=pl.ANY),
        ],
        out_specs=pl.BlockSpec(memory_space=pltpu.VMEM),
        scratch_shapes=[
            pltpu.VMEM(x.shape, x.dtype),
            pltpu.VMEM(s.shape, s.dtype),
            pltpu.SemaphoreType.DMA((2 * len(CHUNKS),)),
            pltpu.VMEM((UNITS, keep, BLOCK), jnp.bfloat16),
            pltpu.VMEM((keep, unit), jnp.bfloat16),
            pltpu.VMEM((*cut, rows, width), jnp.float32),
            *recv_one,
            *recv_two,
            *held_one,
            *held_two,
            pltpu.VMEM((cut[0], 2, share if share % 8 == 0 else rows, width), jnp.float32),
            pltpu.SemaphoreType.DMA((copies,)),
            pltpu.SemaphoreType.DMA((copies,)),
            pltpu.SemaphoreType.DMA((cut[0] * 4,)),
            pltpu.SemaphoreType.DMA((cut[0] * 4,)),
        ],
        compiler_params=pltpu.CompilerParams(
            collective_id=0, has_side_effects=True, vmem_limit_bytes=60 << 20
        ),
    )(kept.reshape(-1, BLOCK), x, s)
    return out.reshape(share, -1, BLOCK).transpose(1, 0, 2).reshape(-1, share * BLOCK)


def solution(mesh):
    placed = (P("trace", "param"), P("param"), P())
    return jax.shard_map(
        per_device,
        mesh=mesh,
        in_specs=placed,
        out_specs=P(None, ("param", "trace")),
        check_vma=False,
    )
```

```python
import functools

import jax
import jax.numpy as jnp
from jax import lax
from jax.experimental import pallas as pl
from jax.experimental.pallas import tpu as pltpu
from jax.sharding import PartitionSpec as P

D = 4096
BLOCK = 128
UNITS = 16
CHUNKS = (1, 2, 3, 4, 6)
BANDS = 4
EARLY = 4
PIECES = 1
SHORT_TWO = 2
SHORT_THREE = 3
MESH = pl.DeviceIdType.MESH


def parity(value, bits):
    shift = 1 << (bits - 1).bit_length()
    while shift > 1:
        shift //= 2
        value = value ^ (value >> shift)
    return value & 1


def sign_of(value, bits):
    return (1 - 2 * parity(value, bits)).astype(jnp.float32).astype(jnp.bfloat16)


def bit_sign(value, bit):
    return (1 - 2 * ((value >> (bit.bit_length() - 1)) & 1)).astype(jnp.float32).astype(jnp.bfloat16)


def cut_of(groups):
    bits = groups.bit_length() - 1
    minor = bits // 3
    return 2 ** (bits - 2 * minor), 2 ** minor, 2 ** minor


def chunk_copies(k, x_hbm, s_hbm, x_ref, s_ref, load_sem):
    unit = s_ref.shape[0] // UNITS
    traces = x_ref.shape[0] // s_ref.shape[0]
    low, size = sum(CHUNKS[:k]) * unit, CHUNKS[k] * unit
    return (
        pltpu.make_async_copy(
            x_hbm.at[pl.ds(low * traces, size * traces)], x_ref.at[pl.ds(low * traces, size * traces)],
            load_sem.at[2 * k],
        ),
        pltpu.make_async_copy(
            s_hbm.at[pl.ds(low, size)], s_ref.at[pl.ds(low, size)], load_sem.at[2 * k + 1]
        ),
    )


def visit_order(count):
    return [0, count - 1, *range(1, count - 1)] if count > 1 else [0]


def parts_of(count):
    early = [(j, 0, 1) for j in range(count // 2)]
    return early + [(j, n, PIECES) for n in range(PIECES) for j in range(count // 2, count)]


def fill_tables(kept_ref, low_ref, high_ref, order, minor):
    unit = low_ref.shape[1]
    kept = jnp.concatenate(
        [jnp.broadcast_to(kept_ref[n:n + 1, :], (BLOCK, BLOCK)).T for n in order], axis=0
    )
    grid = kept.reshape(len(order), minor, minor, -1, BLOCK)
    kept = jnp.where(lax.axis_index("trace") == 0, grid.transpose(0, 2, 1, 3, 4), grid).reshape(kept.shape)
    lane = lax.broadcasted_iota(jnp.int32, kept.shape, 1)
    tables = [sign_of(kept & lane, 7)]
    while len(tables) * BLOCK < unit:
        bit = bit_sign(kept, len(tables) * BLOCK)
        tables += [table * bit for table in tables]
    for k, table in enumerate(tables):
        low_ref[:, k * BLOCK:(k + 1) * BLOCK] = table
    region = UNITS * unit
    own = (kept >> (region.bit_length() - 1)) & lax.axis_index("param")
    highs = [sign_of(own, 8)]
    while len(highs) < UNITS:
        bit = bit_sign(kept, len(highs) * unit)
        highs += [high * bit for high in highs]
    for n, high in enumerate(highs):
        high_ref[n] = high


def load_chunk(k, loads, x_ref, s_ref):
    unit = s_ref.shape[0] // UNITS
    traces = x_ref.shape[0] // s_ref.shape[0]
    for copy in loads:
        copy.wait()
    low, size = sum(CHUNKS[:k]) * unit, CHUNKS[k] * unit
    sign = (2 * s_ref[pl.ds(low, size), :] - 1).astype(jnp.float32).astype(jnp.bfloat16)
    return jnp.concatenate(
        [x_ref[pl.ds(low * traces + t, size, stride=traces), :] * sign for t in range(traces)], axis=1
    )


def add_chunk(band, bands, k, signed, low_ref, high_ref, sums):
    unit = low_ref.shape[1]
    size = low_ref.shape[0] // bands
    rows = slice(band * size, (band + 1) * size)
    first = sum(CHUNKS[:k])
    table = jnp.concatenate(
        [
            low_ref[rows, :] * jnp.concatenate([high_ref[n, rows, :]] * (unit // BLOCK), axis=1)
            for n in range(first, first + CHUNKS[k])
        ],
        axis=1,
    )
    part = jnp.dot(table, signed, preferred_element_type=jnp.float32)
    if k == 0:
        sums[rows, :] = part
    else:
        sums[rows, :] += part


def fused_kernel(
    cut, kept_ref, x_hbm, s_hbm, o_ref, x_ref, s_ref, load_sem, high_ref, low_ref, sums_ref, recv_one, recv_two,
    held_one, held_two, fin_ref, one_send, one_recv, two_send, two_recv, same_send, same_recv, cross_send, cross_recv,
    short_one_ref, short_held_ref, short_two_ref, short_last_ref, short_fin_ref, short_send, short_recv
):
    loads = [chunk_copies(k, x_hbm, s_hbm, x_ref, s_ref, load_sem) for k in range(len(CHUNKS))]
    for pair in loads:
        for copy in pair:
            copy.start()

    own = lax.axis_index("param")
    core = lax.axis_index("trace")
    spans = (cut[1] * cut[2], cut[2], 1)
    place = tuple((own // spans[d]) % cut[d] for d in range(3))

    def peer(d, offset):
        there = lax.rem(place[d] + offset, cut[d])
        return there, own + (there - place[d]) * spans[d]

    at_first = jnp.where(core == 0, place[2], place[1])
    at_second = jnp.where(core == 0, place[1], place[2])
    span_first = jnp.where(core == 0, spans[2], spans[1])
    span_second = jnp.where(core == 0, spans[1], spans[2])
    minor = cut[1]

    barrier = pltpu.get_barrier_semaphore()
    greeted = []
    for d in range(3):
        for offset in range(1, cut[d]):
            for other in range(2):
                greeted.append({"param": peer(d, offset)[1], "trace": 1 - core if other else core})
    greeted.append({"param": own, "trace": 1 - core})
    for device in greeted:
        pl.semaphore_signal(barrier, inc=1, device_id=device, device_id_type=MESH)

    rows, width = sums_ref.shape[3], sums_ref.shape[4]
    keep = kept_ref.shape[0] * BLOCK
    sums = sums_ref.reshape(keep, width)

    visit = visit_order(cut[0])
    at = sum(n * (place[0] == visit[n]).astype(jnp.int32) for n in range(cut[0]))
    parts = parts_of(cut[0])

    def remote(src, dst, sent, received, device):
        return pltpu.make_async_remote_copy(
            src_ref=src, dst_ref=dst, send_sem=sent, recv_sem=received, device_id=device, device_id_type=MESH
        )

    wide = width - BLOCK
    short = pl.ds(wide, BLOCK)

    def lanes(part):
        return pl.ds(part[1] * wide // part[2], wide // part[2])

    def stage_one(n):
        j, cols = parts[n][0], lanes(parts[n])
        for offset in range(1, minor):
            there = lax.rem(at_first + offset, minor)
            remote(
                sums_ref.at[j, there, :, :, cols], recv_one.at[j, offset - 1, :, :, cols], one_send, one_recv.at[n],
                {"param": own + (there - at_first) * span_first},
            ).start()

    def stage_two(n):
        j, cols = parts[n][0], lanes(parts[n])
        landed = recv_one.at[j, :, :, :, cols]
        remote(landed, landed, one_send, one_recv.at[n], {"trace": 1 - core}).wait_recv()
        total = sums_ref[j, at_first, :, :, cols]
        for offset in range(1, minor):
            total = total + recv_one[j, offset - 1, :, :, cols]
        held_one[j, :, :, cols] = total
        for offset in range(1, minor):
            there = lax.rem(at_second + offset, minor)
            remote(
                held_one.at[j, there, :, cols], recv_two.at[j, offset - 1, :, cols], two_send, two_recv.at[n],
                {"param": own + (there - at_second) * span_second},
            ).start()

    share = rows // 2
    whole = share % 8 != 0

    def short_one(n):
        mine = place[0] == visit[n]

        @pl.when(jnp.logical_not(mine))
        def _():
            slot = lax.rem(place[0] - visit[n] + cut[0], cut[0]) - 1
            remote(
                sums_ref.at[n, :, :, :, short], short_one_ref.at[slot], short_send.at[0], short_recv.at[0],
                {"param": own + (visit[n] - place[0]) * spans[0]},
            ).start()

    def short_two():
        remote(short_one_ref, short_one_ref, short_send.at[0], short_recv.at[0], {"trace": 1 - core}).wait_recv()
        total = sums_ref[at, :, :, :, short]
        for slot in range(cut[0] - 1):
            total = total + short_one_ref[slot]
        short_held_ref[...] = total
        for offset in range(1, minor):
            there = lax.rem(at_first + offset, minor)
            remote(
                short_held_ref.at[there], short_two_ref.at[offset - 1], short_send.at[1], short_recv.at[1],
                {"param": own + (there - at_first) * span_first},
            ).start()

    def short_three():
        remote(short_two_ref, short_two_ref, short_send.at[1], short_recv.at[1], {"trace": 1 - core}).wait_recv()
        total = short_held_ref[at_first]
        for offset in range(1, minor):
            total = total + short_two_ref[offset - 1]
        short_last_ref[...] = total

        def rows_of(index, to_core):
            return short_last_ref.at[index, slice(None) if whole else pl.ds(to_core * share, share)]

        there_ref = short_fin_ref.at[at_second, core]
        for offset in range(minor):
            there = lax.rem(at_second + offset, minor)
            target = own + (there - at_second) * span_second
            if offset:
                remote(
                    rows_of(there, core), there_ref, short_send.at[2], short_recv.at[2],
                    {"param": target, "trace": core},
                ).start()
            remote(
                rows_of(there, 1 - core), there_ref, short_send.at[3], short_recv.at[3],
                {"param": target, "trace": 1 - core},
            ).start()
        for c in range(2):
            @pl.when(core == c)
            def _():
                kept_rows = short_last_ref.at[at_second]
                short_fin_ref[at_second, c] = kept_rows[...] if whole else kept_rows[c * share:(c + 1) * share]

    def stage_three(n):
        j, cols = parts[n][0], lanes(parts[n])
        landed = recv_two.at[j, :, :, cols]
        remote(landed, landed, two_send, two_recv.at[n], {"trace": 1 - core}).wait_recv()
        total = held_one[j, at_second, :, cols]
        for offset in range(1, minor):
            total = total + recv_two[j, offset - 1, :, cols]
        held_two[j, :, cols] = total
        mine = place[0] == visit[j]
        target = own + (visit[j] - place[0]) * spans[0]

        def rows_of(to_core):
            return held_two.at[j, slice(None) if whole else pl.ds(to_core * share, share), cols]

        there = fin_ref.at[place[0], core, :, cols]

        @pl.when(jnp.logical_not(mine))
        def _():
            remote(rows_of(core), there, same_send, same_recv, {"param": target, "trace": core}).start()

        remote(rows_of(1 - core), there, cross_send, cross_recv, {"param": target, "trace": 1 - core}).start()

    fill_tables(kept_ref, low_ref, high_ref, visit, minor)
    late = len(CHUNKS) - 1
    for k in range(late - 1):
        signed = load_chunk(k, loads[k], x_ref, s_ref)
        add_chunk(0, 1, k, signed, low_ref, high_ref, sums)
    ends = []
    for k in (late - 1, late):
        ends.append(load_chunk(k, loads[k], x_ref, s_ref))
        for band in range(EARLY if k < late else 1):
            add_chunk(band, BANDS, k, ends[-1], low_ref, high_ref, sums)
    pl.semaphore_wait(barrier, len(greeted))
    stage_one(0)
    short_one(0)
    for band in range(1, BANDS):
        for k in (late - 1, late):
            if k == late or band >= EARLY:
                add_chunk(band, BANDS, k, ends[k - late + 1], low_ref, high_ref, sums)
        if (band + 1) * cut[0] % BANDS == 0:
            j = (band + 1) * cut[0] // BANDS - 1
            if j == 1:
                stage_one(1)
            short_one(j)
    ahead = 2
    for step in range(len(parts) + 1):
        if step < len(parts):
            stage_two(step)
            if ahead < len(parts):
                stage_one(ahead)
                ahead += 1
        if step == SHORT_TWO:
            short_two()
        if step == SHORT_THREE:
            short_three()
        if step >= 1:
            stage_three(step - 1)

    for c in range(2):
        @pl.when(core == c)
        def _():
            fin_ref[place[0], c] = held_two[at] if whole else held_two[at, c * share:(c + 1) * share]

    short_same, short_cross = short_fin_ref.at[0:minor - 1, 0], short_fin_ref.at[:, 0]
    self_same, self_cross = fin_ref.at[0:cut[0] - 1, 0], fin_ref.at[:, 0]
    remote(self_same, self_same, same_send, same_recv, {"trace": 1 - core}).wait_recv()
    remote(self_cross, self_cross, cross_send, cross_recv, {"trace": 1 - core}).wait_recv()
    remote(short_same, short_same, short_send.at[2], short_recv.at[2], {"trace": 1 - core}).wait_recv()
    remote(short_cross, short_cross, short_send.at[3], short_recv.at[3], {"trace": 1 - core}).wait_recv()
    both = []
    for c in range(2):
        total = fin_ref[0, c]
        for z in range(1, cut[0]):
            total = total + fin_ref[z, c]
        last = short_fin_ref[0, c]
        for n in range(1, minor):
            last = last + short_fin_ref[n, c]
        total = jnp.concatenate([total, last], axis=1)
        if whole:
            total = jnp.where(core == 0, total[0:share], total[share:2 * share])
        both.append(total)
    local = width // BLOCK
    for c in range(2):
        for t in range(local):
            o_ref[pl.ds(c * local + t, share, stride=2 * local), :] = both[c][:, t * BLOCK:(t + 1) * BLOCK]
    index = lax.broadcasted_iota(jnp.int32, (BLOCK, BLOCK), 0) & lax.broadcasted_iota(jnp.int32, (BLOCK, BLOCK), 1)
    table = (1 - 2 * parity(index, 7)).astype(jnp.float32) * (1.0 / D)
    o_ref[...] = jnp.dot(
        o_ref[...], table, precision=lax.Precision.HIGHEST, preferred_element_type=jnp.float32
    )
    remote(recv_one, recv_one, one_send, one_recv.at[0], {"trace": 1 - core}).wait_send()
    remote(recv_two, recv_two, two_send, two_recv.at[0], {"trace": 1 - core}).wait_send()
    remote(self_same, self_same, same_send, same_recv, {"trace": 1 - core}).wait_send()
    remote(self_cross, self_cross, cross_send, cross_recv, {"trace": 1 - core}).wait_send()
    for n, ref in enumerate((short_one_ref, short_two_ref, short_same, short_cross)):
        remote(ref, ref, short_send.at[n], short_recv.at[n], {"trace": 1 - core}).wait_send()


def per_device(grads, signs, kept):
    traces, local_size = grads.shape
    groups = lax.axis_size("param")
    keep, width = kept.shape[0], traces * BLOCK
    blocks = local_size // BLOCK
    unit = blocks // UNITS
    x = grads.reshape(traces, blocks, BLOCK).transpose(1, 0, 2).reshape(blocks * traces, BLOCK)
    s = signs.reshape(blocks, BLOCK)
    cut = cut_of(groups)
    rows = keep // groups
    share = rows // 2
    wide = width - BLOCK
    out = pl.pallas_call(
        functools.partial(fused_kernel, cut),
        out_shape=jax.ShapeDtypeStruct((share * 2 * width // BLOCK, BLOCK), jnp.float32),
        in_specs=[
            pl.BlockSpec(memory_space=pltpu.VMEM),
            pl.BlockSpec(memory_space=pl.ANY),
            pl.BlockSpec(memory_space=pl.ANY),
        ],
        out_specs=pl.BlockSpec(memory_space=pltpu.VMEM),
        scratch_shapes=[
            pltpu.VMEM(x.shape, x.dtype),
            pltpu.VMEM(s.shape, s.dtype),
            pltpu.SemaphoreType.DMA((2 * len(CHUNKS),)),
            pltpu.VMEM((UNITS, keep, BLOCK), jnp.bfloat16),
            pltpu.VMEM((keep, unit), jnp.bfloat16),
            pltpu.VMEM((*cut, rows, width), jnp.float32),
            pltpu.VMEM((cut[0], cut[1] - 1, cut[1], rows, wide), jnp.float32),
            pltpu.VMEM((cut[0], cut[1] - 1, rows, wide), jnp.float32),
            pltpu.VMEM((cut[0], cut[1], rows, wide), jnp.float32),
            pltpu.VMEM((cut[0], rows, wide), jnp.float32),
            pltpu.VMEM((cut[0], 2, share if share % 8 == 0 else rows, wide), jnp.float32),
            pltpu.SemaphoreType.DMA,
            pltpu.SemaphoreType.DMA((len(parts_of(cut[0])),)),
            pltpu.SemaphoreType.DMA,
            pltpu.SemaphoreType.DMA((len(parts_of(cut[0])),)),
            pltpu.SemaphoreType.DMA,
            pltpu.SemaphoreType.DMA,
            pltpu.SemaphoreType.DMA,
            pltpu.SemaphoreType.DMA,
            pltpu.VMEM((cut[0] - 1, cut[1], cut[2], rows, BLOCK), jnp.float32),
            pltpu.VMEM((cut[1], cut[2], rows, BLOCK), jnp.float32),
            pltpu.VMEM((cut[1] - 1, cut[2], rows, BLOCK), jnp.float32),
            pltpu.VMEM((cut[1], rows, BLOCK), jnp.float32),
            pltpu.VMEM((cut[1], 2, share if share % 8 == 0 else rows, BLOCK), jnp.float32),
            pltpu.SemaphoreType.DMA((4,)),
            pltpu.SemaphoreType.DMA((4,)),
        ],
        compiler_params=pltpu.CompilerParams(
            collective_id=0, has_side_effects=True, vmem_limit_bytes=60 << 20
        ),
    )(kept.reshape(-1, BLOCK), x, s)
    return out.reshape(share, -1, BLOCK).transpose(1, 0, 2).reshape(-1, share * BLOCK)


def solution(mesh):
    placed = (P("trace", "param"), P("param"), P())
    return jax.shard_map(
        per_device,
        mesh=mesh,
        in_specs=placed,
        out_specs=P(None, ("param", "trace")),
        check_vma=False,
    )
```

```python
import functools

import jax
import jax.numpy as jnp
from jax import lax
from jax.experimental import pallas as pl
from jax.experimental.pallas import tpu as pltpu
from jax.sharding import PartitionSpec as P

D = 4096
BLOCK = 128
UNITS = 16
CHUNKS = (1, 2, 4, 6, 3)
BANDS = 4
EARLY = 1
PIECES = 1
SHORT_TWO = 2
SHORT_THREE = 3
MESH = pl.DeviceIdType.MESH


def parity(value, bits):
    shift = 1 << (bits - 1).bit_length()
    while shift > 1:
        shift //= 2
        value = value ^ (value >> shift)
    return value & 1


def sign_of(value, bits):
    return (1 - 2 * parity(value, bits)).astype(jnp.float32).astype(jnp.bfloat16)


def bit_sign(value, bit):
    return (1 - 2 * ((value >> (bit.bit_length() - 1)) & 1)).astype(jnp.float32).astype(jnp.bfloat16)


def cut_of(groups):
    bits = groups.bit_length() - 1
    minor = bits // 3
    return 2 ** (bits - 2 * minor), 2 ** minor, 2 ** minor


def chunk_copies(k, x_hbm, s_hbm, x_ref, s_ref, load_sem):
    unit = s_ref.shape[0] // UNITS
    traces = x_ref.shape[0] // s_ref.shape[0]
    low, size = sum(CHUNKS[:k]) * unit, CHUNKS[k] * unit
    return (
        pltpu.make_async_copy(
            x_hbm.at[pl.ds(low * traces, size * traces)], x_ref.at[pl.ds(low * traces, size * traces)],
            load_sem.at[2 * k],
        ),
        pltpu.make_async_copy(
            s_hbm.at[pl.ds(low, size)], s_ref.at[pl.ds(low, size)], load_sem.at[2 * k + 1]
        ),
    )


def visit_order(count):
    return [0, count - 1, *range(1, count - 1)] if count > 1 else [0]


def parts_of(count):
    early = [(j, 0, 1) for j in range(count // 2)]
    return early + [(j, n, PIECES) for n in range(PIECES) for j in range(count // 2, count)]


def fill_tables(kept_ref, low_ref, high_ref, order, minor):
    unit = low_ref.shape[1]
    kept = jnp.concatenate(
        [jnp.broadcast_to(kept_ref[n:n + 1, :], (BLOCK, BLOCK)).T for n in order], axis=0
    )
    grid = kept.reshape(len(order), minor, minor, -1, BLOCK)
    kept = jnp.where(lax.axis_index("trace") == 0, grid.transpose(0, 2, 1, 3, 4), grid).reshape(kept.shape)
    lane = lax.broadcasted_iota(jnp.int32, kept.shape, 1)
    tables = [sign_of(kept & lane, 7)]
    while len(tables) * BLOCK < unit:
        bit = bit_sign(kept, len(tables) * BLOCK)
        tables += [table * bit for table in tables]
    for k, table in enumerate(tables):
        low_ref[:, k * BLOCK:(k + 1) * BLOCK] = table
    region = UNITS * unit
    own = (kept >> (region.bit_length() - 1)) & lax.axis_index("param")
    highs = [sign_of(own, 8)]
    while len(highs) < UNITS:
        bit = bit_sign(kept, len(highs) * unit)
        highs += [high * bit for high in highs]
    for n, high in enumerate(highs):
        high_ref[n] = high


def load_chunk(k, loads, x_ref, s_ref):
    unit = s_ref.shape[0] // UNITS
    traces = x_ref.shape[0] // s_ref.shape[0]
    for copy in loads:
        copy.wait()
    low, size = sum(CHUNKS[:k]) * unit, CHUNKS[k] * unit
    sign = (2 * s_ref[pl.ds(low, size), :] - 1).astype(jnp.float32).astype(jnp.bfloat16)
    return jnp.concatenate(
        [x_ref[pl.ds(low * traces + t, size, stride=traces), :] * sign for t in range(traces)], axis=1
    )


def add_chunk(band, bands, k, signed, low_ref, high_ref, sums):
    unit = low_ref.shape[1]
    size = low_ref.shape[0] // bands
    rows = slice(band * size, (band + 1) * size)
    first = sum(CHUNKS[:k])
    table = jnp.concatenate(
        [
            low_ref[rows, :] * jnp.concatenate([high_ref[n, rows, :]] * (unit // BLOCK), axis=1)
            for n in range(first, first + CHUNKS[k])
        ],
        axis=1,
    )
    part = jnp.dot(table, signed, preferred_element_type=jnp.float32)
    if k == 0:
        sums[rows, :] = part
    else:
        sums[rows, :] += part


def fused_kernel(
    cut, kept_ref, x_hbm, s_hbm, o_ref, x_ref, s_ref, load_sem, high_ref, low_ref, sums_ref, recv_one, recv_two,
    held_one, held_two, fin_ref, one_send, one_recv, two_send, two_recv, same_send, same_recv, cross_send, cross_recv,
    short_one_ref, short_held_ref, short_two_ref, short_last_ref, short_fin_ref, short_send, short_recv
):
    loads = [chunk_copies(k, x_hbm, s_hbm, x_ref, s_ref, load_sem) for k in range(len(CHUNKS))]
    for pair in loads:
        for copy in pair:
            copy.start()

    own = lax.axis_index("param")
    core = lax.axis_index("trace")
    spans = (cut[1] * cut[2], cut[2], 1)
    place = tuple((own // spans[d]) % cut[d] for d in range(3))

    def peer(d, offset):
        there = lax.rem(place[d] + offset, cut[d])
        return there, own + (there - place[d]) * spans[d]

    at_first = jnp.where(core == 0, place[2], place[1])
    at_second = jnp.where(core == 0, place[1], place[2])
    span_first = jnp.where(core == 0, spans[2], spans[1])
    span_second = jnp.where(core == 0, spans[1], spans[2])
    minor = cut[1]

    barrier = pltpu.get_barrier_semaphore()
    greeted = []
    for d in range(3):
        for offset in range(1, cut[d]):
            for other in range(2):
                greeted.append({"param": peer(d, offset)[1], "trace": 1 - core if other else core})
    greeted.append({"param": own, "trace": 1 - core})
    for device in greeted:
        pl.semaphore_signal(barrier, inc=1, device_id=device, device_id_type=MESH)

    rows, width = sums_ref.shape[3], sums_ref.shape[4]
    keep = kept_ref.shape[0] * BLOCK
    sums = sums_ref.reshape(keep, width)

    visit = visit_order(cut[0])
    at = sum(n * (place[0] == visit[n]).astype(jnp.int32) for n in range(cut[0]))
    parts = parts_of(cut[0])

    def remote(src, dst, sent, received, device):
        return pltpu.make_async_remote_copy(
            src_ref=src, dst_ref=dst, send_sem=sent, recv_sem=received, device_id=device, device_id_type=MESH
        )

    wide = width - BLOCK
    short = pl.ds(wide, BLOCK)

    def lanes(part):
        return pl.ds(part[1] * wide // part[2], wide // part[2])

    def stage_one(n):
        j, cols = parts[n][0], lanes(parts[n])
        for offset in range(1, minor):
            there = lax.rem(at_first + offset, minor)
            remote(
                sums_ref.at[j, there, :, :, cols], recv_one.at[j, offset - 1, :, :, cols], one_send, one_recv.at[n],
                {"param": own + (there - at_first) * span_first},
            ).start()

    def stage_two(n):
        j, cols = parts[n][0], lanes(parts[n])
        landed = recv_one.at[j, :, :, :, cols]
        remote(landed, landed, one_send, one_recv.at[n], {"trace": 1 - core}).wait_recv()
        total = sums_ref[j, at_first, :, :, cols]
        for offset in range(1, minor):
            total = total + recv_one[j, offset - 1, :, :, cols]
        held_one[j, :, :, cols] = total
        for offset in range(1, minor):
            there = lax.rem(at_second + offset, minor)
            remote(
                held_one.at[j, there, :, cols], recv_two.at[j, offset - 1, :, cols], two_send, two_recv.at[n],
                {"param": own + (there - at_second) * span_second},
            ).start()

    share = rows // 2
    whole = share % 8 != 0

    def short_one(n):
        mine = place[0] == visit[n]

        @pl.when(jnp.logical_not(mine))
        def _():
            slot = lax.rem(place[0] - visit[n] + cut[0], cut[0]) - 1
            remote(
                sums_ref.at[n, :, :, :, short], short_one_ref.at[slot], short_send.at[0], short_recv.at[0],
                {"param": own + (visit[n] - place[0]) * spans[0]},
            ).start()

    def short_two():
        remote(short_one_ref, short_one_ref, short_send.at[0], short_recv.at[0], {"trace": 1 - core}).wait_recv()
        total = sums_ref[at, :, :, :, short]
        for slot in range(cut[0] - 1):
            total = total + short_one_ref[slot]
        short_held_ref[...] = total
        for offset in range(1, minor):
            there = lax.rem(at_first + offset, minor)
            remote(
                short_held_ref.at[there], short_two_ref.at[offset - 1], short_send.at[1], short_recv.at[1],
                {"param": own + (there - at_first) * span_first},
            ).start()

    def short_three():
        remote(short_two_ref, short_two_ref, short_send.at[1], short_recv.at[1], {"trace": 1 - core}).wait_recv()
        total = short_held_ref[at_first]
        for offset in range(1, minor):
            total = total + short_two_ref[offset - 1]
        short_last_ref[...] = total

        def rows_of(index, to_core):
            return short_last_ref.at[index, slice(None) if whole else pl.ds(to_core * share, share)]

        there_ref = short_fin_ref.at[at_second, core]
        for offset in range(minor):
            there = lax.rem(at_second + offset, minor)
            target = own + (there - at_second) * span_second
            if offset:
                remote(
                    rows_of(there, core), there_ref, short_send.at[2], short_recv.at[2],
                    {"param": target, "trace": core},
                ).start()
            remote(
                rows_of(there, 1 - core), there_ref, short_send.at[3], short_recv.at[3],
                {"param": target, "trace": 1 - core},
            ).start()
        for c in range(2):
            @pl.when(core == c)
            def _():
                kept_rows = short_last_ref.at[at_second]
                short_fin_ref[at_second, c] = kept_rows[...] if whole else kept_rows[c * share:(c + 1) * share]

    def stage_three(n):
        j, cols = parts[n][0], lanes(parts[n])
        landed = recv_two.at[j, :, :, cols]
        remote(landed, landed, two_send, two_recv.at[n], {"trace": 1 - core}).wait_recv()
        total = held_one[j, at_second, :, cols]
        for offset in range(1, minor):
            total = total + recv_two[j, offset - 1, :, cols]
        held_two[j, :, cols] = total
        mine = place[0] == visit[j]
        target = own + (visit[j] - place[0]) * spans[0]

        def rows_of(to_core):
            return held_two.at[j, slice(None) if whole else pl.ds(to_core * share, share), cols]

        there = fin_ref.at[place[0], core, :, cols]

        @pl.when(jnp.logical_not(mine))
        def _():
            remote(rows_of(core), there, same_send, same_recv, {"param": target, "trace": core}).start()

        remote(rows_of(1 - core), there, cross_send, cross_recv, {"param": target, "trace": 1 - core}).start()

    fill_tables(kept_ref, low_ref, high_ref, visit, minor)
    late = len(CHUNKS) - 1
    for k in range(late - 1):
        signed = load_chunk(k, loads[k], x_ref, s_ref)
        add_chunk(0, 1, k, signed, low_ref, high_ref, sums)
    ends = []
    for k in (late - 1, late):
        ends.append(load_chunk(k, loads[k], x_ref, s_ref))
        for band in range(EARLY if k < late else 1):
            add_chunk(band, BANDS, k, ends[-1], low_ref, high_ref, sums)
    pl.semaphore_wait(barrier, len(greeted))
    stage_one(0)
    short_one(0)
    for band in range(1, BANDS):
        for k in (late - 1, late):
            if k == late or band >= EARLY:
                add_chunk(band, BANDS, k, ends[k - late + 1], low_ref, high_ref, sums)
        if (band + 1) * cut[0] % BANDS == 0:
            j = (band + 1) * cut[0] // BANDS - 1
            if j == 1:
                stage_one(1)
            short_one(j)
    ahead = 2
    for step in range(len(parts) + 1):
        if step < len(parts):
            stage_two(step)
            if ahead < len(parts):
                stage_one(ahead)
                ahead += 1
        if step == SHORT_TWO:
            short_two()
        if step == SHORT_THREE:
            short_three()
        if step >= 1:
            stage_three(step - 1)

    for c in range(2):
        @pl.when(core == c)
        def _():
            fin_ref[place[0], c] = held_two[at] if whole else held_two[at, c * share:(c + 1) * share]

    short_same, short_cross = short_fin_ref.at[0:minor - 1, 0], short_fin_ref.at[:, 0]
    self_same, self_cross = fin_ref.at[0:cut[0] - 1, 0], fin_ref.at[:, 0]
    remote(self_same, self_same, same_send, same_recv, {"trace": 1 - core}).wait_recv()
    remote(self_cross, self_cross, cross_send, cross_recv, {"trace": 1 - core}).wait_recv()
    remote(short_same, short_same, short_send.at[2], short_recv.at[2], {"trace": 1 - core}).wait_recv()
    remote(short_cross, short_cross, short_send.at[3], short_recv.at[3], {"trace": 1 - core}).wait_recv()
    both = []
    for c in range(2):
        total = fin_ref[0, c]
        for z in range(1, cut[0]):
            total = total + fin_ref[z, c]
        last = short_fin_ref[0, c]
        for n in range(1, minor):
            last = last + short_fin_ref[n, c]
        total = jnp.concatenate([total, last], axis=1)
        if whole:
            total = jnp.where(core == 0, total[0:share], total[share:2 * share])
        both.append(total)
    local = width // BLOCK
    for c in range(2):
        for t in range(local):
            o_ref[pl.ds(c * local + t, share, stride=2 * local), :] = both[c][:, t * BLOCK:(t + 1) * BLOCK]
    remote(recv_one, recv_one, one_send, one_recv.at[0], {"trace": 1 - core}).wait_send()
    remote(recv_two, recv_two, two_send, two_recv.at[0], {"trace": 1 - core}).wait_send()
    remote(self_same, self_same, same_send, same_recv, {"trace": 1 - core}).wait_send()
    remote(self_cross, self_cross, cross_send, cross_recv, {"trace": 1 - core}).wait_send()
    for n, ref in enumerate((short_one_ref, short_two_ref, short_same, short_cross)):
        remote(ref, ref, short_send.at[n], short_recv.at[n], {"trace": 1 - core}).wait_send()


def per_device(grads, signs, kept):
    traces, local_size = grads.shape
    groups = lax.axis_size("param")
    keep, width = kept.shape[0], traces * BLOCK
    blocks = local_size // BLOCK
    unit = blocks // UNITS
    x = grads.reshape(traces, blocks, BLOCK).transpose(1, 0, 2).reshape(blocks * traces, BLOCK)
    s = signs.reshape(blocks, BLOCK)
    cut = cut_of(groups)
    rows = keep // groups
    share = rows // 2
    wide = width - BLOCK
    out = pl.pallas_call(
        functools.partial(fused_kernel, cut),
        out_shape=jax.ShapeDtypeStruct((share * 2 * width // BLOCK, BLOCK), jnp.float32),
        in_specs=[
            pl.BlockSpec(memory_space=pltpu.VMEM),
            pl.BlockSpec(memory_space=pl.ANY),
            pl.BlockSpec(memory_space=pl.ANY),
        ],
        out_specs=pl.BlockSpec(memory_space=pltpu.VMEM),
        scratch_shapes=[
            pltpu.VMEM(x.shape, x.dtype),
            pltpu.VMEM(s.shape, s.dtype),
            pltpu.SemaphoreType.DMA((2 * len(CHUNKS),)),
            pltpu.VMEM((UNITS, keep, BLOCK), jnp.bfloat16),
            pltpu.VMEM((keep, unit), jnp.bfloat16),
            pltpu.VMEM((*cut, rows, width), jnp.float32),
            pltpu.VMEM((cut[0], cut[1] - 1, cut[1], rows, wide), jnp.float32),
            pltpu.VMEM((cut[0], cut[1] - 1, rows, wide), jnp.float32),
            pltpu.VMEM((cut[0], cut[1], rows, wide), jnp.float32),
            pltpu.VMEM((cut[0], rows, wide), jnp.float32),
            pltpu.VMEM((cut[0], 2, share if share % 8 == 0 else rows, wide), jnp.float32),
            pltpu.SemaphoreType.DMA,
            pltpu.SemaphoreType.DMA((len(parts_of(cut[0])),)),
            pltpu.SemaphoreType.DMA,
            pltpu.SemaphoreType.DMA((len(parts_of(cut[0])),)),
            pltpu.SemaphoreType.DMA,
            pltpu.SemaphoreType.DMA,
            pltpu.SemaphoreType.DMA,
            pltpu.SemaphoreType.DMA,
            pltpu.VMEM((cut[0] - 1, cut[1], cut[2], rows, BLOCK), jnp.float32),
            pltpu.VMEM((cut[1], cut[2], rows, BLOCK), jnp.float32),
            pltpu.VMEM((cut[1] - 1, cut[2], rows, BLOCK), jnp.float32),
            pltpu.VMEM((cut[1], rows, BLOCK), jnp.float32),
            pltpu.VMEM((cut[1], 2, share if share % 8 == 0 else rows, BLOCK), jnp.float32),
            pltpu.SemaphoreType.DMA((4,)),
            pltpu.SemaphoreType.DMA((4,)),
        ],
        compiler_params=pltpu.CompilerParams(
            collective_id=0, has_side_effects=True, vmem_limit_bytes=51 << 20
        ),
    )(kept.reshape(-1, BLOCK), x, s)
    index = lax.broadcasted_iota(jnp.int32, (BLOCK, BLOCK), 0) & lax.broadcasted_iota(jnp.int32, (BLOCK, BLOCK), 1)
    table = (1 - 2 * parity(index, 7)).astype(jnp.float32) * (1.0 / D)
    out = jnp.dot(out, table, precision=lax.Precision.HIGHEST, preferred_element_type=jnp.float32)
    return out.reshape(share, -1, BLOCK).transpose(1, 0, 2).reshape(-1, share * BLOCK)


def solution(mesh):
    placed = (P("trace", "param"), P("param"), P())
    return jax.shard_map(
        per_device,
        mesh=mesh,
        in_specs=placed,
        out_specs=P(None, ("param", "trace")),
        check_vma=False,
    )
```

```python
import functools

import jax
import jax.numpy as jnp
from jax import lax
from jax.experimental import pallas as pl
from jax.experimental.pallas import tpu as pltpu
from jax.sharding import PartitionSpec as P

D = 4096
BLOCK = 128
UNITS = 16
CHUNKS = (1, 2, 4, 6, 3)
BANDS = 4
EARLY = 1
PIECES = 1
SHORT_TWO = 2
SHORT_THREE = 4
MESH = pl.DeviceIdType.MESH


def parity(value, bits):
    shift = 1 << (bits - 1).bit_length()
    while shift > 1:
        shift //= 2
        value = value ^ (value >> shift)
    return value & 1


def sign_of(value, bits):
    return (1 - 2 * parity(value, bits)).astype(jnp.float32).astype(jnp.bfloat16)


def bit_sign(value, bit):
    return (1 - 2 * ((value >> (bit.bit_length() - 1)) & 1)).astype(jnp.float32).astype(jnp.bfloat16)


def cut_of(groups):
    bits = groups.bit_length() - 1
    minor = bits // 3
    return 2 ** (bits - 2 * minor), 2 ** minor, 2 ** minor


def chunk_copies(k, x_hbm, s_hbm, x_ref, s_ref, load_sem):
    unit = s_ref.shape[0] // UNITS
    traces = x_ref.shape[0] // s_ref.shape[0]
    low, size = sum(CHUNKS[:k]) * unit, CHUNKS[k] * unit
    return (
        pltpu.make_async_copy(
            x_hbm.at[pl.ds(low * traces, size * traces)], x_ref.at[pl.ds(low * traces, size * traces)],
            load_sem.at[2 * k],
        ),
        pltpu.make_async_copy(
            s_hbm.at[pl.ds(low, size)], s_ref.at[pl.ds(low, size)], load_sem.at[2 * k + 1]
        ),
    )


def visit_order(count):
    return [0, 2, 1, 3] if count == 4 else list(range(count))


def parts_of(count):
    early = [(j, 0, 1) for j in range(count // 2)]
    return early + [(j, n, PIECES) for n in range(PIECES) for j in range(count // 2, count)]


def fill_tables(kept_ref, low_ref, high_ref, order, minor):
    unit = low_ref.shape[1]
    kept = jnp.concatenate(
        [jnp.broadcast_to(kept_ref[n:n + 1, :], (BLOCK, BLOCK)).T for n in order], axis=0
    )
    grid = kept.reshape(len(order), minor, minor, -1, BLOCK)
    kept = jnp.where(lax.axis_index("trace") == 0, grid.transpose(0, 2, 1, 3, 4), grid).reshape(kept.shape)
    lane = lax.broadcasted_iota(jnp.int32, kept.shape, 1)
    tables = [sign_of(kept & lane, 7)]
    while len(tables) * BLOCK < unit:
        bit = bit_sign(kept, len(tables) * BLOCK)
        tables += [table * bit for table in tables]
    for k, table in enumerate(tables):
        low_ref[:, k * BLOCK:(k + 1) * BLOCK] = table
    region = UNITS * unit
    own = (kept >> (region.bit_length() - 1)) & lax.axis_index("param")
    highs = [sign_of(own, 8)]
    while len(highs) < UNITS:
        bit = bit_sign(kept, len(highs) * unit)
        highs += [high * bit for high in highs]
    for n, high in enumerate(highs):
        high_ref[n] = high


def load_chunk(k, loads, x_ref, s_ref):
    unit = s_ref.shape[0] // UNITS
    traces = x_ref.shape[0] // s_ref.shape[0]
    for copy in loads:
        copy.wait()
    low, size = sum(CHUNKS[:k]) * unit, CHUNKS[k] * unit
    sign = (2 * s_ref[pl.ds(low, size), :] - 1).astype(jnp.float32).astype(jnp.bfloat16)
    return jnp.concatenate(
        [x_ref[pl.ds(low * traces + t, size, stride=traces), :] * sign for t in range(traces)], axis=1
    )


def add_chunk(band, bands, k, signed, low_ref, high_ref, sums):
    unit = low_ref.shape[1]
    size = low_ref.shape[0] // bands
    rows = slice(band * size, (band + 1) * size)
    first = sum(CHUNKS[:k])
    table = jnp.concatenate(
        [
            low_ref[rows, :] * jnp.concatenate([high_ref[n, rows, :]] * (unit // BLOCK), axis=1)
            for n in range(first, first + CHUNKS[k])
        ],
        axis=1,
    )
    part = jnp.dot(table, signed, preferred_element_type=jnp.float32)
    if k == 0:
        sums[rows, :] = part
    else:
        sums[rows, :] += part


def fused_kernel(
    cut, kept_ref, x_hbm, s_hbm, o_ref, x_ref, s_ref, load_sem, high_ref, low_ref, sums_ref, recv_one, recv_two,
    held_one, held_two, fin_ref, one_send, one_recv, two_send, two_recv, same_send, same_recv, cross_send, cross_recv,
    short_one_ref, short_held_ref, short_two_ref, short_last_ref, short_fin_ref, short_send, short_recv
):
    loads = [chunk_copies(k, x_hbm, s_hbm, x_ref, s_ref, load_sem) for k in range(len(CHUNKS))]
    for pair in loads:
        for copy in pair:
            copy.start()

    own = lax.axis_index("param")
    core = lax.axis_index("trace")
    spans = (cut[1] * cut[2], cut[2], 1)
    place = tuple((own // spans[d]) % cut[d] for d in range(3))

    def peer(d, offset):
        there = lax.rem(place[d] + offset, cut[d])
        return there, own + (there - place[d]) * spans[d]

    at_first = jnp.where(core == 0, place[2], place[1])
    at_second = jnp.where(core == 0, place[1], place[2])
    span_first = jnp.where(core == 0, spans[2], spans[1])
    span_second = jnp.where(core == 0, spans[1], spans[2])
    minor = cut[1]

    barrier = pltpu.get_barrier_semaphore()
    greeted = []
    for d in range(3):
        for offset in range(1, cut[d]):
            for other in range(2):
                greeted.append({"param": peer(d, offset)[1], "trace": 1 - core if other else core})
    greeted.append({"param": own, "trace": 1 - core})
    for device in greeted:
        pl.semaphore_signal(barrier, inc=1, device_id=device, device_id_type=MESH)

    rows, width = sums_ref.shape[3], sums_ref.shape[4]
    keep = kept_ref.shape[0] * BLOCK
    sums = sums_ref.reshape(keep, width)

    visit = visit_order(cut[0])
    at = sum(n * (place[0] == visit[n]).astype(jnp.int32) for n in range(cut[0]))
    parts = parts_of(cut[0])

    def remote(src, dst, sent, received, device):
        return pltpu.make_async_remote_copy(
            src_ref=src, dst_ref=dst, send_sem=sent, recv_sem=received, device_id=device, device_id_type=MESH
        )

    wide = width - BLOCK
    short = pl.ds(wide, BLOCK)

    def lanes(part):
        return pl.ds(part[1] * wide // part[2], wide // part[2])

    def stage_one(n):
        j, cols = parts[n][0], lanes(parts[n])
        for offset in range(1, minor):
            there = lax.rem(at_first + offset, minor)
            remote(
                sums_ref.at[j, there, :, :, cols], recv_one.at[j, offset - 1, :, :, cols], one_send, one_recv.at[n],
                {"param": own + (there - at_first) * span_first},
            ).start()

    def stage_two(n):
        j, cols = parts[n][0], lanes(parts[n])
        landed = recv_one.at[j, :, :, :, cols]
        remote(landed, landed, one_send, one_recv.at[n], {"trace": 1 - core}).wait_recv()
        total = sums_ref[j, at_first, :, :, cols]
        for offset in range(1, minor):
            total = total + recv_one[j, offset - 1, :, :, cols]
        held_one[j, :, :, cols] = total
        for offset in range(1, minor):
            there = lax.rem(at_second + offset, minor)
            remote(
                held_one.at[j, there, :, cols], recv_two.at[j, offset - 1, :, cols], two_send, two_recv.at[n],
                {"param": own + (there - at_second) * span_second},
            ).start()

    share = rows // 2
    whole = share % 8 != 0

    def short_one(n):
        mine = place[0] == visit[n]

        @pl.when(jnp.logical_not(mine))
        def _():
            slot = lax.rem(place[0] - visit[n] + cut[0], cut[0]) - 1
            remote(
                sums_ref.at[n, :, :, :, short], short_one_ref.at[slot], short_send.at[0], short_recv.at[0],
                {"param": own + (visit[n] - place[0]) * spans[0]},
            ).start()

    def short_two():
        remote(short_one_ref, short_one_ref, short_send.at[0], short_recv.at[0], {"trace": 1 - core}).wait_recv()
        total = sums_ref[at, :, :, :, short]
        for slot in range(cut[0] - 1):
            total = total + short_one_ref[slot]
        short_held_ref[...] = total
        for offset in range(1, minor):
            there = lax.rem(at_first + offset, minor)
            remote(
                short_held_ref.at[there], short_two_ref.at[offset - 1], short_send.at[1], short_recv.at[1],
                {"param": own + (there - at_first) * span_first},
            ).start()

    def short_three():
        remote(short_two_ref, short_two_ref, short_send.at[1], short_recv.at[1], {"trace": 1 - core}).wait_recv()
        total = short_held_ref[at_first]
        for offset in range(1, minor):
            total = total + short_two_ref[offset - 1]
        short_last_ref[...] = total

        def rows_of(index, to_core):
            return short_last_ref.at[index, slice(None) if whole else pl.ds(to_core * share, share)]

        there_ref = short_fin_ref.at[at_second, core]
        for offset in range(minor):
            there = lax.rem(at_second + offset, minor)
            target = own + (there - at_second) * span_second
            if offset:
                remote(
                    rows_of(there, core), there_ref, short_send.at[2], short_recv.at[2],
                    {"param": target, "trace": core},
                ).start()
            remote(
                rows_of(there, 1 - core), there_ref, short_send.at[3], short_recv.at[3],
                {"param": target, "trace": 1 - core},
            ).start()
        for c in range(2):
            @pl.when(core == c)
            def _():
                kept_rows = short_last_ref.at[at_second]
                short_fin_ref[at_second, c] = kept_rows[...] if whole else kept_rows[c * share:(c + 1) * share]

    def stage_three(n):
        j, cols = parts[n][0], lanes(parts[n])
        landed = recv_two.at[j, :, :, cols]
        remote(landed, landed, two_send, two_recv.at[n], {"trace": 1 - core}).wait_recv()
        total = held_one[j, at_second, :, cols]
        for offset in range(1, minor):
            total = total + recv_two[j, offset - 1, :, cols]
        held_two[j, :, cols] = total
        mine = place[0] == visit[j]
        target = own + (visit[j] - place[0]) * spans[0]

        def rows_of(to_core):
            return held_two.at[j, slice(None) if whole else pl.ds(to_core * share, share), cols]

        there = fin_ref.at[place[0], core, :, cols]

        @pl.when(jnp.logical_not(mine))
        def _():
            remote(rows_of(core), there, same_send, same_recv, {"param": target, "trace": core}).start()

        remote(rows_of(1 - core), there, cross_send, cross_recv, {"param": target, "trace": 1 - core}).start()

    fill_tables(kept_ref, low_ref, high_ref, visit, minor)
    late = len(CHUNKS) - 1
    for k in range(late - 1):
        signed = load_chunk(k, loads[k], x_ref, s_ref)
        add_chunk(0, 1, k, signed, low_ref, high_ref, sums)
    ends = []
    for k in (late - 1, late):
        ends.append(load_chunk(k, loads[k], x_ref, s_ref))
        for band in range(EARLY if k < late else 1):
            add_chunk(band, BANDS, k, ends[-1], low_ref, high_ref, sums)
    pl.semaphore_wait(barrier, len(greeted))
    stage_one(0)
    short_one(0)
    for band in range(1, BANDS):
        for k in (late - 1, late):
            if k == late or band >= EARLY:
                add_chunk(band, BANDS, k, ends[k - late + 1], low_ref, high_ref, sums)
        if (band + 1) * cut[0] % BANDS == 0:
            j = (band + 1) * cut[0] // BANDS - 1
            if j == 1:
                stage_one(1)
            short_one(j)
    stage_one(2)
    stage_one(3)
    ahead = 4
    for step in range(len(parts) + 1):
        if step < len(parts):
            stage_two(step)
            if ahead < len(parts):
                stage_one(ahead)
                ahead += 1
        if step == SHORT_TWO:
            short_two()
        if step == SHORT_THREE:
            short_three()
        if step >= 1:
            stage_three(step - 1)

    for c in range(2):
        @pl.when(core == c)
        def _():
            fin_ref[place[0], c] = held_two[at] if whole else held_two[at, c * share:(c + 1) * share]

    short_same, short_cross = short_fin_ref.at[0:minor - 1, 0], short_fin_ref.at[:, 0]
    self_same, self_cross = fin_ref.at[0:cut[0] - 1, 0], fin_ref.at[:, 0]
    remote(self_same, self_same, same_send, same_recv, {"trace": 1 - core}).wait_recv()
    remote(self_cross, self_cross, cross_send, cross_recv, {"trace": 1 - core}).wait_recv()
    remote(short_same, short_same, short_send.at[2], short_recv.at[2], {"trace": 1 - core}).wait_recv()
    remote(short_cross, short_cross, short_send.at[3], short_recv.at[3], {"trace": 1 - core}).wait_recv()
    both = []
    for c in range(2):
        total = fin_ref[0, c]
        for z in range(1, cut[0]):
            total = total + fin_ref[z, c]
        last = short_fin_ref[0, c]
        for n in range(1, minor):
            last = last + short_fin_ref[n, c]
        total = jnp.concatenate([total, last], axis=1)
        if whole:
            total = jnp.where(core == 0, total[0:share], total[share:2 * share])
        both.append(total)
    local = width // BLOCK
    for c in range(2):
        for t in range(local):
            o_ref[pl.ds(c * local + t, share, stride=2 * local), :] = both[c][:, t * BLOCK:(t + 1) * BLOCK]
    remote(recv_one, recv_one, one_send, one_recv.at[0], {"trace": 1 - core}).wait_send()
    remote(recv_two, recv_two, two_send, two_recv.at[0], {"trace": 1 - core}).wait_send()
    remote(self_same, self_same, same_send, same_recv, {"trace": 1 - core}).wait_send()
    remote(self_cross, self_cross, cross_send, cross_recv, {"trace": 1 - core}).wait_send()
    for n, ref in enumerate((short_one_ref, short_two_ref, short_same, short_cross)):
        remote(ref, ref, short_send.at[n], short_recv.at[n], {"trace": 1 - core}).wait_send()


def per_device(grads, signs, kept):
    traces, local_size = grads.shape
    groups = lax.axis_size("param")
    keep, width = kept.shape[0], traces * BLOCK
    blocks = local_size // BLOCK
    unit = blocks // UNITS
    x = grads.reshape(traces, blocks, BLOCK).transpose(1, 0, 2).reshape(blocks * traces, BLOCK)
    s = signs.reshape(blocks, BLOCK)
    cut = cut_of(groups)
    rows = keep // groups
    share = rows // 2
    wide = width - BLOCK
    out = pl.pallas_call(
        functools.partial(fused_kernel, cut),
        out_shape=jax.ShapeDtypeStruct((share * 2 * width // BLOCK, BLOCK), jnp.float32),
        in_specs=[
            pl.BlockSpec(memory_space=pltpu.VMEM),
            pl.BlockSpec(memory_space=pl.ANY),
            pl.BlockSpec(memory_space=pl.ANY),
        ],
        out_specs=pl.BlockSpec(memory_space=pltpu.VMEM),
        scratch_shapes=[
            pltpu.VMEM(x.shape, x.dtype),
            pltpu.VMEM(s.shape, s.dtype),
            pltpu.SemaphoreType.DMA((2 * len(CHUNKS),)),
            pltpu.VMEM((UNITS, keep, BLOCK), jnp.bfloat16),
            pltpu.VMEM((keep, unit), jnp.bfloat16),
            pltpu.VMEM((*cut, rows, width), jnp.float32),
            pltpu.VMEM((cut[0], cut[1] - 1, cut[1], rows, wide), jnp.float32),
            pltpu.VMEM((cut[0], cut[1] - 1, rows, wide), jnp.float32),
            pltpu.VMEM((cut[0], cut[1], rows, wide), jnp.float32),
            pltpu.VMEM((cut[0], rows, wide), jnp.float32),
            pltpu.VMEM((cut[0], 2, share if share % 8 == 0 else rows, wide), jnp.float32),
            pltpu.SemaphoreType.DMA,
            pltpu.SemaphoreType.DMA((len(parts_of(cut[0])),)),
            pltpu.SemaphoreType.DMA,
            pltpu.SemaphoreType.DMA((len(parts_of(cut[0])),)),
            pltpu.SemaphoreType.DMA,
            pltpu.SemaphoreType.DMA,
            pltpu.SemaphoreType.DMA,
            pltpu.SemaphoreType.DMA,
            pltpu.VMEM((cut[0] - 1, cut[1], cut[2], rows, BLOCK), jnp.float32),
            pltpu.VMEM((cut[1], cut[2], rows, BLOCK), jnp.float32),
            pltpu.VMEM((cut[1] - 1, cut[2], rows, BLOCK), jnp.float32),
            pltpu.VMEM((cut[1], rows, BLOCK), jnp.float32),
            pltpu.VMEM((cut[1], 2, share if share % 8 == 0 else rows, BLOCK), jnp.float32),
            pltpu.SemaphoreType.DMA((4,)),
            pltpu.SemaphoreType.DMA((4,)),
        ],
        compiler_params=pltpu.CompilerParams(
            collective_id=0, has_side_effects=True, vmem_limit_bytes=51 << 20
        ),
    )(kept.reshape(-1, BLOCK), x, s)
    index = lax.broadcasted_iota(jnp.int32, (BLOCK, BLOCK), 0) & lax.broadcasted_iota(jnp.int32, (BLOCK, BLOCK), 1)
    table = (1 - 2 * parity(index, 7)).astype(jnp.float32) * (1.0 / D)
    out = jnp.dot(out, table, precision=lax.Precision.HIGHEST, preferred_element_type=jnp.float32)
    return out.reshape(share, -1, BLOCK).transpose(1, 0, 2).reshape(-1, share * BLOCK)


def solution(mesh):
    placed = (P("trace", "param"), P("param"), P())
    return jax.shard_map(
        per_device,
        mesh=mesh,
        in_specs=placed,
        out_specs=P(None, ("param", "trace")),
        check_vma=False,
    )
```
